32 devices in a mesh: patch: 8 (over z, x), lev: 4 (over y, core).
Axes of the slice: x: 2, y: 2, z: 4, core: 2. Of those that a mesh axis runs over, the one named last changes fastest.
Arguments:
- tracer_field: float32 [80, 3, 16384], P('lev', None, 'patch'), may hold values from -6 to 6
- send_coarse1: int32 [8, 2, 128], P('patch'), may hold values from 0 to 1023
- send_detail1: int32 [8, 2, 128], P('patch'), may hold values from 0 to 1023
- send_coarse2: int32 [8, 2, 64], P('patch'), may hold values from 0 to 511
- send_detail2: int32 [8, 2, 64], P('patch'), may hold values from 0 to 511
- predict_links1: int32 [8, 8192], P(None, 'patch'), may hold values from 0 to 1279
- predict_weights1: float32 [8, 8192], P(None, 'patch'), may hold values from 0.02 to 0.22
- update_links1: int32 [8, 8192], P(None, 'patch'), may hold values from 0 to 1279
- update_weights1: float32 [8, 8192], P(None, 'patch'), may hold values from 0.02 to 0.14
- predict_links2: int32 [8, 4096], P(None, 'patch'), may hold values from 0 to 639
- predict_weights2: float32 [8, 4096], P(None, 'patch'), may hold values from 0.02 to 0.22
- update_links2: int32 [8, 4096], P(None, 'patch'), may hold values from 0 to 639
- update_weights2: float32 [8, 4096], P(None, 'patch'), may hold values from 0.02 to 0.14
Outputs:
- coefficients: float32 [80, 3, 16384], P(None, None, ('patch', 'lev'))
The draws below stay inside these ranges and needn't reach their ends.
Inputs may be any that keep to these rules, and one draw needn't show every extreme that they name: `send_coarse1`: row lists index a patch's own coarse or detail rows of that level. `predict_links1`: links index the patch's own rows first, then the 128 rows from the left neighbour, then the 128 from the right. `predict_links2`: links index the patch's own rows first, then the 64 rows from the left neighbour, then the 64 from the right.
All inputs are finite; a program needn't handle non-finite values.
Results may differ from the reference program's by a relative error of at most 0.00007.
Values sent between devices are 32-bit elements; how exact they have to be, the bound alone decides.
A program may use at most 64 MiB of HBM per device.

```python
import jax
import jax.numpy as jnp
from jax import lax

LEVELS = 80
TRACERS = 3
NBRS = 8
CELL_DEV = 2048
PATCHES = 8
CELLS = 16384
HALO1 = 128
HALO2 = 64


def touch_ends(entries, own_key, smallest, high):
    longest = entries.shape.index(max(entries.shape))
    spots = []
    for shift in (0, 1):
        where = [jax.random.randint(jax.random.fold_in(own_key, axis), (), 0, length) for axis, length in enumerate(entries.shape)]
        where[longest] = (where[longest] + shift) % entries.shape[longest]
        spots.append(tuple(where))
    return entries.at[spots[0]].set(smallest).at[spots[1]].set(high)


def shard_levels(key, shape, cuts, least, top_value):
    loudness = 1.0
    for axis_at, shards_of in cuts:
        heights = jax.random.uniform(jax.random.fold_in(jax.random.fold_in(key, 6), axis_at), (shards_of,), jnp.float32, least / len(cuts), top_value / len(cuts))
        loudness = loudness * jnp.repeat(jnp.exp(heights), shape[axis_at] // shards_of).reshape((-1,) + (1,) * (len(shape) - 1 - axis_at))
    return loudness


def centred(own_key, extent, scale, bound, split=(), held_as=jnp.bfloat16):
    drawn = jax.random.normal(own_key, extent, jnp.float32) * scale
    if len(split) > 0:
        drawn = shard_levels(own_key, extent, split, -0.22, 0.18) * drawn
    return jnp.clip(drawn, min=-bound, max=bound).astype(held_as)


def setup_inputs(seed: int = 0) -> dict:
    splits = jax.random.split(jax.random.key(seed), 14)
    return {
        "tracer_field": centred(splits[0], (LEVELS, TRACERS, CELLS), 1.0, 6.0, ((0, 4), (2, 8)), jnp.float32),
        "send_coarse1": touch_ends(jax.random.randint(splits[1], (PATCHES, 2, HALO1), 0, CELL_DEV // 2), jax.random.fold_in(splits[1], 1), 0, (CELL_DEV // 2) - 1).astype(jnp.int32),
        "send_detail1": touch_ends(jax.random.randint(splits[2], (PATCHES, 2, HALO1), 0, CELL_DEV // 2), jax.random.fold_in(splits[2], 1), 0, (CELL_DEV // 2) - 1).astype(jnp.int32),
        "send_coarse2": touch_ends(jax.random.randint(splits[3], (PATCHES, 2, HALO2), 0, CELL_DEV // 4), jax.random.fold_in(splits[3], 1), 0, (CELL_DEV // 4) - 1).astype(jnp.int32),
        "send_detail2": touch_ends(jax.random.randint(splits[4], (PATCHES, 2, HALO2), 0, CELL_DEV // 4), jax.random.fold_in(splits[4], 1), 0, (CELL_DEV // 4) - 1).astype(jnp.int32),
        "predict_links1": touch_ends(jax.random.randint(splits[5], (NBRS, CELLS // 2), 0, CELL_DEV // 2 + CELL_DEV // 8), jax.random.fold_in(splits[5], 1), 0, (CELL_DEV // 2 + CELL_DEV // 8) - 1).astype(jnp.int32),
        "predict_weights1": jnp.clip(0.02 + 0.2 * jax.random.uniform(splits[6], (NBRS, CELLS // 2), jnp.float32) ** shard_levels(splits[6], (NBRS, CELLS // 2), ((1, 8),), -0.2, 0.2), 0.02, 0.22),
        "update_links1": touch_ends(jax.random.randint(splits[7], (NBRS, CELLS // 2), 0, CELL_DEV // 2 + CELL_DEV // 8), jax.random.fold_in(splits[7], 1), 0, (CELL_DEV // 2 + CELL_DEV // 8) - 1).astype(jnp.int32),
        "update_weights1": jnp.clip(0.02 + 0.12000000104308128 * jax.random.uniform(splits[8], (NBRS, CELLS // 2), jnp.float32) ** shard_levels(splits[8], (NBRS, CELLS // 2), ((1, 8),), -0.2, 0.2), 0.02, 0.14),
        "predict_links2": touch_ends(jax.random.randint(splits[9], (NBRS, CELLS // 4), 0, CELL_DEV // 4 + CELL_DEV // 16), jax.random.fold_in(splits[9], 1), 0, (CELL_DEV // 4 + CELL_DEV // 16) - 1).astype(jnp.int32),
        "predict_weights2": jnp.clip(0.02 + 0.2 * jax.random.uniform(splits[10], (NBRS, CELLS // 4), jnp.float32) ** shard_levels(splits[10], (NBRS, CELLS // 4), ((1, 8),), -0.2, 0.2), 0.02, 0.22),
        "update_links2": touch_ends(jax.random.randint(splits[11], (NBRS, CELLS // 4), 0, CELL_DEV // 4 + CELL_DEV // 16), jax.random.fold_in(splits[11], 1), 0, (CELL_DEV // 4 + CELL_DEV // 16) - 1).astype(jnp.int32),
        "update_weights2": jnp.clip(0.02 + 0.12000000104308128 * jax.random.uniform(splits[12], (NBRS, CELLS // 4), jnp.float32) ** shard_levels(splits[12], (NBRS, CELLS // 4), ((1, 8),), -0.2, 0.2), 0.02, 0.14),
    }


def cosine_table(length):
    rows = jnp.arange(length).astype(jnp.float32)[:, None]
    columns = jnp.arange(length).astype(jnp.float32)[None, :]
    matrix = jnp.cos(jnp.pi * (columns + 0.5) * rows / length) * jnp.sqrt(2.0 / length)
    first = jnp.where(rows == 0.0, jnp.sqrt(0.5), 1.0)
    return (matrix * first).astype(jnp.float32)

def extend(values, send_rows):
    patch_index = jnp.arange(values.shape[2])[:, None]
    first = values[:, :, patch_index, send_rows[:, 0, :]]
    second = values[:, :, patch_index, send_rows[:, 1, :]]
    from_left = jnp.roll(second, 1, axis=2)
    from_right = jnp.roll(first, -1, axis=2)
    return jnp.concatenate([values, from_left, from_right], axis=3)

def weighted(extended, links, weights):
    patch_index = jnp.arange(extended.shape[2])[:, None]
    total = jnp.zeros(extended.shape[:3] + (links.shape[2],), jnp.float32)
    for neighbour in range(links.shape[0]):
        total = total + weights[neighbour] * extended[:, :, patch_index, links[neighbour]]
    return total

def lift(values, send_coarse, send_detail, predict_links, predict_weights, update_links, update_weights):
    patches = values.shape[2]
    half_cells = values.shape[3] // 2
    fine_part = values[..., :half_cells]
    coarse = values[..., half_cells:]
    plinks = predict_links.reshape(predict_links.shape[0], patches, half_cells)
    pweights = predict_weights.reshape(predict_weights.shape[0], patches, half_cells)
    ulinks = update_links.reshape(update_links.shape[0], patches, half_cells)
    uweights = update_weights.reshape(update_weights.shape[0], patches, half_cells)
    detail = fine_part - weighted(extend(coarse, send_coarse), plinks, pweights)
    smooth = coarse + weighted(extend(detail, send_detail), ulinks, uweights)
    return (detail, smooth)

def reference(tracer_field, send_coarse1, send_detail1, send_coarse2, send_detail2, predict_links1, predict_weights1, update_links1, update_weights1, predict_links2, predict_weights2, update_links2, update_weights2):
    values = tracer_field.reshape(LEVELS, TRACERS, PATCHES, CELL_DEV)
    detail1, smooth1 = lift(values, send_coarse1, send_detail1, predict_links1, predict_weights1, update_links1, update_weights1)
    detail2, smooth2 = lift(smooth1, send_coarse2, send_detail2, predict_links2, predict_weights2, update_links2, update_weights2)
    bands = jnp.concatenate([detail1, detail2, smooth2], axis=3).reshape(LEVELS, TRACERS, CELLS)
    table = cosine_table(LEVELS)
    return jnp.einsum('km,mtc->ktc', table, bands, precision=lax.Precision.HIGHEST)
```

```python
import functools

import jax
import jax.numpy as jnp
import ml_dtypes
import numpy as np
from jax import lax
from jax.experimental import pallas as pl
from jax.experimental.pallas import tpu as pltpu
from jax.sharding import PartitionSpec as P

LANES = 128
SUB = 8
MESH = pl.DeviceIdType.MESH


def cosine_table(length):
    rows = np.arange(length, dtype=np.float64)[:, None]
    columns = np.arange(length, dtype=np.float64)[None, :]
    matrix = np.cos(np.pi * (columns + 0.5) * rows / length) * np.sqrt(2.0 / length)
    matrix[0] *= np.sqrt(0.5)
    return matrix


def spread_table(levels, tracers, groups, padded):
    own = levels // groups
    table = cosine_table(levels).reshape(levels, groups, own)
    wide = np.zeros((tracers, levels, groups, padded))
    for t in range(tracers):
        wide[t, :, :, t * own : (t + 1) * own] = table
    wide = wide.reshape(levels * tracers, groups * padded).astype(np.float32)
    high = wide.astype(ml_dtypes.bfloat16)
    low = (wide - high.astype(np.float32)).astype(ml_dtypes.bfloat16)
    return high, low


def halves(x):
    high = x.astype(jnp.bfloat16)
    low = (x - high.astype(jnp.float32)).astype(jnp.bfloat16)
    return high, low


def build(links, weights, merged, w_high, w_low, first, count, blocks):
    slots = links.shape[0]
    groups = -(-blocks // SUB)

    def column(tile, _):
        cols = pl.ds(pl.multiple_of(first + tile * LANES, LANES), LANES)
        lane = []
        block = []
        weight = []
        for k in range(slots):
            link = jnp.broadcast_to(links[k : k + 1, cols], (SUB, LANES))
            lane.append(link & (LANES - 1))
            block.append(link >> 7)
            weight.append(jnp.broadcast_to(weights[k : k + 1, cols], (SUB, LANES)))
        which = lax.broadcasted_iota(jnp.int32, (SUB, LANES), 0)
        for g in range(groups):
            placed = []
            for k in range(slots):
                mine = jnp.where(block[k] == which + g * SUB, weight[k], 0.0)
                total = mine
                for j in range(k):
                    total = total + jnp.where(lane[j] == lane[k], placed[j], 0.0)
                placed.append(mine)
                merged[k, g * SUB : (g + 1) * SUB, :] = total
        lane2 = [jnp.concatenate([v, v], axis=0) for v in lane]

        def strip(s, _):
            rows16 = lax.broadcasted_iota(jnp.int32, (2 * SUB, LANES), 0) + s * (2 * SUB)
            masks = [lane2[k] == rows16 for k in range(slots)]
            for b in range(blocks):
                total = jnp.zeros((2 * SUB, LANES), jnp.float32)
                for k in range(slots):
                    row = jnp.broadcast_to(merged[k, b : b + 1, :], (2 * SUB, LANES))
                    total = jnp.where(masks[k], row, total)
                high, low = halves(total)
                place = pl.ds(pl.multiple_of(b * LANES + s * (2 * SUB), 2 * SUB), 2 * SUB)
                w_high[place, cols] = high
                w_low[place, cols] = low
            return 0

        lax.fori_loop(0, LANES // (2 * SUB), strip, 0)
        return 0

    lax.fori_loop(0, count // LANES, column, 0)


def picked(source, start, blocks, index, out):
    lane = jnp.broadcast_to(index & (LANES - 1), (SUB, LANES))
    block = jnp.broadcast_to(index >> 7, (SUB, LANES))
    for r in range(source.shape[0] // SUB):
        rows = slice(r * SUB, (r + 1) * SUB)
        got = None
        for b in range(blocks):
            cols = slice(start + b * LANES, start + (b + 1) * LANES)
            t = jnp.take_along_axis(source[rows, cols], lane, axis=1)
            got = t if got is None else jnp.where(block == b, t, got)
        out[rows, :] = got


def put(ext, padded, at, value):
    high, low = halves(value)
    width = value.shape[1]
    ext[0:padded, at : at + width] = high
    ext[padded : 2 * padded, at : at + width] = low


def product(ext, padded, depth, w_high, w_low, cols):
    both = jnp.dot(ext[:, 0:depth], w_high[:, cols], preferred_element_type=jnp.float32)
    rest = jnp.dot(ext[0:padded, 0:depth], w_low[:, cols], preferred_element_type=jnp.float32)
    return both[0:padded] + both[padded : 2 * padded] + rest


def body(
    n_patch, n_lev, levels,
    field, sc1, sd1, sc2, sd2, pl1, pw1, ul1, uw1, pl2, pw2, ul2, uw2, t_high, t_low,
    out,
    xs, ext, merged, p1h, p1l, u1h, u1l, p2h, p2l, u2h, u2l,
    det1, sm1, det2, sm2, hsend, hrecv, gathered, res,
    hs_sem, hr_sem, as_sem, ar_sem,
):
    tracers, own, cells = field.shape
    rows = own * tracers
    padded = xs.shape[0]
    n1 = cells // 2
    n2 = cells // 4
    halo1 = sc1.shape[2]
    halo2 = sc2.shape[2]
    chunk = cells // n_lev
    me = lax.axis_index("lev")
    patch = lax.axis_index("patch")
    left = lax.rem(patch + n_patch - 1, n_patch)
    right = lax.rem(patch + 1, n_patch)

    barrier = pltpu.get_barrier_semaphore()
    for neighbour in (left, right):
        pl.semaphore_signal(barrier, inc=1, device_id={"patch": neighbour}, device_id_type=MESH)
    for d in range(1, n_lev):
        pl.semaphore_signal(
            barrier, inc=1, device_id={"lev": lax.rem(me + d, n_lev)}, device_id_type=MESH
        )

    if padded > rows:
        edge = rows // SUB * SUB
        xs[edge:padded, :] = jnp.zeros((padded - edge, cells), jnp.float32)
    for t in range(tracers):
        xs[t * own : (t + 1) * own, :] = field[t]

    def swap(phase, first_buf, second_buf):
        copies = []
        for side, (buf, to) in enumerate(((second_buf, right), (first_buf, left))):
            copies.append(
                pltpu.make_async_remote_copy(
                    src_ref=buf,
                    dst_ref=hrecv.at[phase, side],
                    send_sem=hs_sem.at[phase, side],
                    recv_sem=hr_sem.at[phase, side],
                    device_id={"patch": to},
                    device_id_type=MESH,
                )
            )
        for c in copies:
            c.start()
        return copies

    def send_one(phase, source, start, blocks, send):
        picked(source, start, blocks, send[0, 0:1, :], hsend.at[phase, 0])
        picked(source, start, blocks, send[0, 1:2, :], hsend.at[phase, 1])

    def send_two(phase, source, start, blocks, send):
        index = jnp.concatenate([send[0, 1:2, :], send[0, 0:1, :]], axis=1)
        picked(source, start, blocks, index, hsend.at[phase, 0])

    def land_one(phase, at):
        put(ext, padded, at, hrecv[phase, 0])
        put(ext, padded, at + halo1, hrecv[phase, 1])

    def land_two(phase, at):
        lanes = lax.broadcasted_iota(jnp.int32, (padded, LANES), 1)
        put(ext, padded, at, jnp.where(lanes < halo2, hrecv[phase, 0], hrecv[phase, 1]))

    outgoing = []

    def scatter(source, base):
        for piece in range(source.shape[1] // chunk):
            d = base // chunk + piece
            part = source.at[:, piece * chunk : (piece + 1) * chunk]
            copy = pltpu.make_async_remote_copy(
                src_ref=part,
                dst_ref=gathered.at[me],
                send_sem=as_sem.at[d],
                recv_sem=ar_sem.at[me],
                device_id={"lev": d},
                device_id_type=MESH,
            )
            outgoing.append((d, copy))

            @pl.when(me != d)
            def _():
                copy.start()

            @pl.when(me == d)
            def _():
                gathered[d] = part[...]

    b1 = n1 // LANES
    b2 = n2 // LANES
    e1 = n1 + 2 * halo1
    e2 = n2 + 2 * halo2
    wide = 256

    send_one(0, xs, n1, b1, sc1)
    pl.semaphore_wait(barrier, 2 + n_lev - 1)
    flight = swap(0, hsend.at[0, 0], hsend.at[0, 1])
    put(ext, padded, 0, xs[:, n1:cells])
    build(pl1, pw1, merged, p1h, p1l, 0, n1, e1 // LANES)
    for c in flight:
        c.wait()
    land_one(0, n1)
    for c in range(0, n1, wide):
        cols = slice(c, c + wide)
        det1[:, cols] = xs[:, cols] - product(ext, padded, e1, p1h, p1l, cols)

    send_one(1, det1, 0, b1, sd1)
    flight = swap(1, hsend.at[1, 0], hsend.at[1, 1])
    scatter(det1, 0)
    put(ext, padded, 0, det1[...])
    build(ul1, uw1, merged, u1h, u1l, n2, n2, e1 // LANES)
    build(pl2, pw2, merged, p2h, p2l, 0, n2, e2 // LANES)
    for c in flight:
        c.wait()
    land_one(1, n1)
    for c in range(n2, n1, wide):
        cols = slice(c, c + wide)
        sm1[:, cols] = xs[:, n1 + c : n1 + c + wide] + product(ext, padded, e1, u1h, u1l, cols)

    send_two(2, sm1, n2, b2, sc2)
    flight = swap(2, hsend.at[2, 0], hsend.at[2, 0])
    build(ul1, uw1, merged, u1h, u1l, 0, n2, e1 // LANES)
    for c in range(0, n2, wide):
        cols = slice(c, c + wide)
        sm1[:, cols] = xs[:, n1 + c : n1 + c + wide] + product(ext, padded, e1, u1h, u1l, cols)
    put(ext, padded, 0, sm1[:, n2:n1])
    for c in flight:
        c.wait()
    land_two(2, n2)
    for c in range(0, n2, wide):
        cols = slice(c, c + wide)
        det2[:, cols] = sm1[:, cols] - product(ext, padded, e2, p2h, p2l, cols)

    send_two(3, det2, 0, b2, sd2)
    flight = swap(3, hsend.at[3, 0], hsend.at[3, 0])
    scatter(det2, n1)
    put(ext, padded, 0, det2[...])
    build(ul2, uw2, merged, u2h, u2l, 0, n2, e2 // LANES)
    for c in flight:
        c.wait()
    land_two(3, n2)
    for c in range(0, n2, wide):
        cols = slice(c, c + wide)
        sm2[:, cols] = sm1[:, n2 + c : n2 + c + wide] + product(ext, padded, e2, u2h, u2l, cols)
    scatter(sm2, n1 + n2)

    for s in range(n_lev):

        @pl.when(me != s)
        def _():
            pltpu.make_async_remote_copy(
                src_ref=gathered.at[s],
                dst_ref=gathered.at[s],
                send_sem=as_sem.at[s],
                recv_sem=ar_sem.at[s],
                device_id={"lev": s},
                device_id_type=MESH,
            ).wait_recv()

    high, low = halves(gathered[...].reshape(n_lev * padded, chunk))
    res[...] = (
        jnp.dot(t_high[...], high, preferred_element_type=jnp.float32)
        + jnp.dot(t_high[...], low, preferred_element_type=jnp.float32)
        + jnp.dot(t_low[...], high, preferred_element_type=jnp.float32)
    )
    for t in range(tracers):
        out[t] = res[t * levels : (t + 1) * levels, :]

    for d, copy in outgoing:

        @pl.when(me != d)
        def _():
            copy.wait_send()


def on_device(n_patch, n_lev, *args):
    field, sc1 = args[0], args[1]
    own, tracers, cells = field.shape
    levels = own * n_lev
    rows = own * tracers
    padded = -(-rows // (2 * SUB)) * (2 * SUB)
    n1, n2 = cells // 2, cells // 4
    e1 = n1 + 2 * sc1.shape[2]
    e2 = n2 + 2 * args[3].shape[2]
    chunk = cells // n_lev
    slots = args[5].shape[0]
    t_high, t_low = spread_table(levels, tracers, n_lev, padded)
    f32, bf16 = jnp.float32, jnp.bfloat16
    result = pl.pallas_call(
        functools.partial(body, n_patch, n_lev, levels),
        out_shape=jax.ShapeDtypeStruct((tracers, levels, chunk), f32),
        in_specs=[pl.BlockSpec(memory_space=pltpu.VMEM)] * 15,
        out_specs=pl.BlockSpec(memory_space=pltpu.VMEM),
        scratch_shapes=[
            pltpu.VMEM((padded, cells), f32),
            pltpu.VMEM((2 * padded, e1), bf16),
            pltpu.VMEM((slots, -(-(e1 // LANES) // SUB) * SUB, LANES), f32),
            pltpu.VMEM((e1, n1), bf16),
            pltpu.VMEM((e1, n1), bf16),
            pltpu.VMEM((e1, n1), bf16),
            pltpu.VMEM((e1, n1), bf16),
            pltpu.VMEM((e2, n2), bf16),
            pltpu.VMEM((e2, n2), bf16),
            pltpu.VMEM((e2, n2), bf16),
            pltpu.VMEM((e2, n2), bf16),
            pltpu.VMEM((padded, n1), f32),
            pltpu.VMEM((padded, n1), f32),
            pltpu.VMEM((padded, n2), f32),
            pltpu.VMEM((padded, n2), f32),
            pltpu.VMEM((4, 2, padded, LANES), f32),
            pltpu.VMEM((4, 2, padded, LANES), f32),
            pltpu.VMEM((n_lev, padded, chunk), f32),
            pltpu.VMEM((levels * tracers, chunk), f32),
            pltpu.SemaphoreType.DMA((4, 2)),
            pltpu.SemaphoreType.DMA((4, 2)),
            pltpu.SemaphoreType.DMA((n_lev,)),
            pltpu.SemaphoreType.DMA((n_lev,)),
        ],
        compiler_params=pltpu.CompilerParams(collective_id=0, has_side_effects=True),
    )(jnp.transpose(field, (1, 0, 2)), *args[1:], jnp.asarray(t_high), jnp.asarray(t_low))
    return jnp.transpose(result, (1, 0, 2))


def solution(mesh):
    in_specs = (P("lev", None, "patch"),)
    in_specs += (P("patch", None, None),) * 4
    in_specs += (P(None, "patch"),) * 8
    out_specs = P(None, None, ("patch", "lev"))
    fn = functools.partial(on_device, mesh.shape["patch"], mesh.shape["lev"])
    return jax.shard_map(
        fn, mesh=mesh, in_specs=in_specs, out_specs=out_specs, check_vma=False
    )
```

```python
import functools

import jax
import jax.numpy as jnp
import ml_dtypes
import numpy as np
from jax import lax
from jax.experimental import pallas as pl
from jax.experimental.pallas import tpu as pltpu
from jax.sharding import PartitionSpec as P

LANES = 128
SUB = 8
MESH = pl.DeviceIdType.MESH


def cosine_table(length):
    rows = np.arange(length, dtype=np.float64)[:, None]
    columns = np.arange(length, dtype=np.float64)[None, :]
    matrix = np.cos(np.pi * (columns + 0.5) * rows / length) * np.sqrt(2.0 / length)
    matrix[0] *= np.sqrt(0.5)
    return matrix


def spread_table(levels, tracers, groups, padded):
    own = levels // groups
    table = cosine_table(levels).reshape(levels, groups, own)
    wide = np.zeros((tracers, levels, groups, padded))
    for t in range(tracers):
        wide[t, :, :, t * own : (t + 1) * own] = table
    wide = wide.reshape(levels * tracers, groups * padded).astype(np.float32)
    high = wide.astype(ml_dtypes.bfloat16)
    low = (wide - high.astype(np.float32)).astype(ml_dtypes.bfloat16)
    return high, low


def halves(x):
    high = x.astype(jnp.bfloat16)
    low = (x - high.astype(jnp.float32)).astype(jnp.bfloat16)
    return high, low


def build(links, weights, merged, w_high, w_low, first, count, blocks):
    slots = links.shape[0]
    groups = -(-blocks // SUB)

    def column(tile, _):
        cols = pl.ds(pl.multiple_of(first + tile * LANES, LANES), LANES)
        lane = []
        block = []
        weight = []
        for k in range(slots):
            link = jnp.broadcast_to(links[k : k + 1, cols], (SUB, LANES))
            lane.append(link & (LANES - 1))
            block.append(link >> 7)
            weight.append(jnp.broadcast_to(weights[k : k + 1, cols], (SUB, LANES)))
        which = lax.broadcasted_iota(jnp.int32, (SUB, LANES), 0)
        for g in range(groups):
            placed = []
            for k in range(slots):
                mine = jnp.where(block[k] == which + g * SUB, weight[k], 0.0)
                total = mine
                for j in range(k):
                    total = total + jnp.where(lane[j] == lane[k], placed[j], 0.0)
                placed.append(mine)
                merged[k, g * SUB : (g + 1) * SUB, :] = total
        lane2 = [jnp.concatenate([v, v], axis=0) for v in lane]

        def strip(s, _):
            rows16 = lax.broadcasted_iota(jnp.int32, (2 * SUB, LANES), 0) + s * (2 * SUB)
            masks = [lane2[k] == rows16 for k in range(slots)]
            for b in range(blocks):
                total = jnp.zeros((2 * SUB, LANES), jnp.float32)
                for k in range(slots):
                    row = jnp.broadcast_to(merged[k, b : b + 1, :], (2 * SUB, LANES))
                    total = jnp.where(masks[k], row, total)
                high, low = halves(total)
                place = pl.ds(pl.multiple_of(b * LANES + s * (2 * SUB), 2 * SUB), 2 * SUB)
                w_high[place, cols] = high
                w_low[place, cols] = low
            return 0

        lax.fori_loop(0, LANES // (2 * SUB), strip, 0)
        return 0

    lax.fori_loop(0, count // LANES, column, 0)


def picked(source, start, blocks, index, out):
    lane = jnp.broadcast_to(index & (LANES - 1), (SUB, LANES))
    block = jnp.broadcast_to(index >> 7, (SUB, LANES))
    for r in range(source.shape[0] // SUB):
        rows = slice(r * SUB, (r + 1) * SUB)
        got = None
        for b in range(blocks):
            cols = slice(start + b * LANES, start + (b + 1) * LANES)
            t = jnp.take_along_axis(source[rows, cols], lane, axis=1)
            got = t if got is None else jnp.where(block == b, t, got)
        out[rows, :] = got


def put(ext, padded, at, value):
    high, low = halves(value)
    width = value.shape[1]
    ext[0:padded, at : at + width] = high
    ext[padded : 2 * padded, at : at + width] = low


def product(ext, padded, span, w_high, w_low, cols):
    k = slice(*span)
    both = jnp.dot(ext[:, k], w_high[k, cols], preferred_element_type=jnp.float32)
    rest = jnp.dot(ext[0:padded, k], w_low[k, cols], preferred_element_type=jnp.float32)
    return both[0:padded] + both[padded : 2 * padded] + rest


def body(
    n_patch, n_lev, levels,
    field, sc1, sd1, sc2, sd2, pl1, pw1, ul1, uw1, pl2, pw2, ul2, uw2,
    gathered,
    xs, ext, merged, p1h, p1l, u1h, u1l, p2h, p2l, u2h, u2l,
    det1, sm1, det2, sm2, hsend, hrecv,
    hs_sem, hr_sem, as_sem, ar_sem,
):
    tracers, own, cells = field.shape
    rows = own * tracers
    padded = xs.shape[0]
    n1 = cells // 2
    n2 = cells // 4
    halo1 = sc1.shape[2]
    halo2 = sc2.shape[2]
    chunk = cells // n_lev
    me = lax.axis_index("lev")
    patch = lax.axis_index("patch")
    left = lax.rem(patch + n_patch - 1, n_patch)
    right = lax.rem(patch + 1, n_patch)

    barrier = pltpu.get_barrier_semaphore()
    for neighbour in (left, right):
        pl.semaphore_signal(barrier, inc=1, device_id={"patch": neighbour}, device_id_type=MESH)
    for d in range(1, n_lev):
        pl.semaphore_signal(
            barrier, inc=1, device_id={"lev": lax.rem(me + d, n_lev)}, device_id_type=MESH
        )

    if padded > rows:
        edge = rows // SUB * SUB
        xs[edge:padded, :] = jnp.zeros((padded - edge, cells), jnp.float32)
    for t in range(tracers):
        xs[t * own : (t + 1) * own, :] = field[t]

    def swap(phase, first_buf, second_buf):
        copies = []
        for side, (buf, to) in enumerate(((second_buf, right), (first_buf, left))):
            copies.append(
                pltpu.make_async_remote_copy(
                    src_ref=buf,
                    dst_ref=hrecv.at[phase, side],
                    send_sem=hs_sem.at[phase, side],
                    recv_sem=hr_sem.at[phase, side],
                    device_id={"patch": to},
                    device_id_type=MESH,
                )
            )
        for c in copies:
            c.start()
        return copies

    def send_one(phase, source, start, blocks, send):
        picked(source, start, blocks, send[0, 0:1, :], hsend.at[phase, 0])
        picked(source, start, blocks, send[0, 1:2, :], hsend.at[phase, 1])

    def send_two(phase, source, start, blocks, send):
        index = jnp.concatenate([send[0, 1:2, :], send[0, 0:1, :]], axis=1)
        picked(source, start, blocks, index, hsend.at[phase, 0])

    def land_one(phase, at):
        put(ext, padded, at, hrecv[phase, 0])
        put(ext, padded, at + halo1, hrecv[phase, 1])

    def land_two(phase, at):
        lanes = lax.broadcasted_iota(jnp.int32, (padded, LANES), 1)
        put(ext, padded, at, jnp.where(lanes < halo2, hrecv[phase, 0], hrecv[phase, 1]))

    outgoing = []

    def scatter(source, base):
        for piece in range(source.shape[1] // chunk):
            d = base // chunk + piece
            part = source.at[:, piece * chunk : (piece + 1) * chunk]
            copy = pltpu.make_async_remote_copy(
                src_ref=part,
                dst_ref=gathered.at[me],
                send_sem=as_sem.at[d],
                recv_sem=ar_sem.at[me],
                device_id={"lev": d},
                device_id_type=MESH,
            )
            outgoing.append((d, copy))

            @pl.when(me != d)
            def _():
                copy.start()

            @pl.when(me == d)
            def _():
                gathered[d] = part[...]

    b1 = n1 // LANES
    b2 = n2 // LANES
    e1 = n1 + 2 * halo1
    e2 = n2 + 2 * halo2
    wide = 256

    def predict(into, start, values, depth, w_high, w_low, n, add):
        for c in range(0, n, wide):
            cols = slice(start + c, start + c + wide)
            got = product(ext, padded, depth, w_high, w_low, cols)
            old = values(cols)
            into[:, cols] = old + got if add else old - got

    def fine1(cols):
        return xs[:, cols]

    def coarse1(cols):
        return xs[:, n1 + cols.start : n1 + cols.stop]

    def fine2(cols):
        return sm1[:, cols]

    def coarse2(cols):
        return sm1[:, n2 + cols.start : n2 + cols.stop]

    def held(ref):
        return lambda cols: ref[:, cols]

    send_one(0, xs, n1, b1, sc1)
    pl.semaphore_wait(barrier, 2 + n_lev - 1)
    flight = swap(0, hsend.at[0, 0], hsend.at[0, 1])
    put(ext, padded, 0, xs[:, n1:cells])
    build(pl1, pw1, merged, p1h, p1l, 0, n1, e1 // LANES)
    predict(det1, 0, fine1, (0, n1), p1h, p1l, n1, False)
    for c in flight:
        c.wait()
    land_one(0, n1)
    predict(det1, 0, held(det1), (n1, e1), p1h, p1l, n1, False)

    send_one(1, det1, 0, b1, sd1)
    flight = swap(1, hsend.at[1, 0], hsend.at[1, 1])
    scatter(det1, 0)
    put(ext, padded, 0, det1[...])
    build(ul1, uw1, merged, u1h, u1l, n2, n2, e1 // LANES)
    predict(sm1, n2, coarse1, (0, n1), u1h, u1l, n2, True)
    build(pl2, pw2, merged, p2h, p2l, 0, n2, e2 // LANES)
    for c in flight:
        c.wait()
    land_one(1, n1)
    predict(sm1, n2, held(sm1), (n1, e1), u1h, u1l, n2, True)

    send_two(2, sm1, n2, b2, sc2)
    flight = swap(2, hsend.at[2, 0], hsend.at[2, 0])
    build(ul1, uw1, merged, u1h, u1l, 0, n2, e1 // LANES)
    predict(sm1, 0, coarse1, (0, e1), u1h, u1l, n2, True)
    put(ext, padded, 0, sm1[:, n2:n1])
    predict(det2, 0, fine2, (0, n2), p2h, p2l, n2, False)
    for c in flight:
        c.wait()
    land_two(2, n2)
    predict(det2, 0, held(det2), (n2, e2), p2h, p2l, n2, False)

    send_two(3, det2, 0, b2, sd2)
    flight = swap(3, hsend.at[3, 0], hsend.at[3, 0])
    scatter(det2, n1)
    put(ext, padded, 0, det2[...])
    build(ul2, uw2, merged, u2h, u2l, 0, n2, e2 // LANES)
    predict(sm2, 0, coarse2, (0, n2), u2h, u2l, n2, True)
    for c in flight:
        c.wait()
    land_two(3, n2)
    predict(sm2, 0, held(sm2), (n2, e2), u2h, u2l, n2, True)
    scatter(sm2, n1 + n2)

    for s in range(n_lev):

        @pl.when(me != s)
        def _():
            pltpu.make_async_remote_copy(
                src_ref=gathered.at[s],
                dst_ref=gathered.at[s],
                send_sem=as_sem.at[s],
                recv_sem=ar_sem.at[s],
                device_id={"lev": s},
                device_id_type=MESH,
            ).wait_recv()

    for d, copy in outgoing:

        @pl.when(me != d)
        def _():
            copy.wait_send()


def transform(gathered, t_high, t_low, out):
    groups, padded, chunk = gathered.shape
    tracers, levels, _ = out.shape
    high, low = halves(gathered[...].reshape(groups * padded, chunk))
    for t in range(tracers):
        rows = slice(t * levels, (t + 1) * levels)
        out[t] = (
            jnp.dot(t_high[rows, :], high, preferred_element_type=jnp.float32)
            + jnp.dot(t_high[rows, :], low, preferred_element_type=jnp.float32)
            + jnp.dot(t_low[rows, :], high, preferred_element_type=jnp.float32)
        )


def on_device(n_patch, n_lev, *args):
    field, sc1 = args[0], args[1]
    own, tracers, cells = field.shape
    levels = own * n_lev
    rows = own * tracers
    padded = -(-rows // (2 * SUB)) * (2 * SUB)
    n1, n2 = cells // 2, cells // 4
    e1 = n1 + 2 * sc1.shape[2]
    e2 = n2 + 2 * args[3].shape[2]
    chunk = cells // n_lev
    slots = args[5].shape[0]
    t_high, t_low = spread_table(levels, tracers, n_lev, padded)
    f32, bf16 = jnp.float32, jnp.bfloat16
    gathered = pl.pallas_call(
        functools.partial(body, n_patch, n_lev, levels),
        out_shape=jax.ShapeDtypeStruct((n_lev, padded, chunk), f32),
        in_specs=[pl.BlockSpec(memory_space=pltpu.VMEM)] * 13,
        out_specs=pl.BlockSpec(memory_space=pltpu.VMEM),
        scratch_shapes=[
            pltpu.VMEM((padded, cells), f32),
            pltpu.VMEM((2 * padded, e1), bf16),
            pltpu.VMEM((slots, -(-(e1 // LANES) // SUB) * SUB, LANES), f32),
            pltpu.VMEM((e1, n1), bf16),
            pltpu.VMEM((e1, n1), bf16),
            pltpu.VMEM((e1, n1), bf16),
            pltpu.VMEM((e1, n1), bf16),
            pltpu.VMEM((e2, n2), bf16),
            pltpu.VMEM((e2, n2), bf16),
            pltpu.VMEM((e2, n2), bf16),
            pltpu.VMEM((e2, n2), bf16),
            pltpu.VMEM((padded, n1), f32),
            pltpu.VMEM((padded, n1), f32),
            pltpu.VMEM((padded, n2), f32),
            pltpu.VMEM((padded, n2), f32),
            pltpu.VMEM((4, 2, padded, LANES), f32),
            pltpu.VMEM((4, 2, padded, LANES), f32),
            pltpu.SemaphoreType.DMA((4, 2)),
            pltpu.SemaphoreType.DMA((4, 2)),
            pltpu.SemaphoreType.DMA((n_lev,)),
            pltpu.SemaphoreType.DMA((n_lev,)),
        ],
        compiler_params=pltpu.CompilerParams(collective_id=0, has_side_effects=True),
    )(jnp.transpose(field, (1, 0, 2)), *args[1:])
    result = pl.pallas_call(
        transform,
        out_shape=jax.ShapeDtypeStruct((tracers, levels, chunk), f32),
        in_specs=[pl.BlockSpec(memory_space=pltpu.VMEM)] * 3,
        out_specs=pl.BlockSpec(memory_space=pltpu.VMEM),
    )(gathered, jnp.asarray(t_high), jnp.asarray(t_low))
    return jnp.transpose(result, (1, 0, 2))


def solution(mesh):
    in_specs = (P("lev", None, "patch"),)
    in_specs += (P("patch", None, None),) * 4
    in_specs += (P(None, "patch"),) * 8
    out_specs = P(None, None, ("patch", "lev"))
    fn = functools.partial(on_device, mesh.shape["patch"], mesh.shape["lev"])
    return jax.shard_map(
        fn, mesh=mesh, in_specs=in_specs, out_specs=out_specs, check_vma=False
    )
```

```python
import functools

import jax
import jax.numpy as jnp
import ml_dtypes
import numpy as np
from jax import lax
from jax.experimental import pallas as pl
from jax.experimental.pallas import tpu as pltpu
from jax.sharding import PartitionSpec as P

LANES = 128
SUB = 8
MESH = pl.DeviceIdType.MESH


def cosine_table(length):
    rows = np.arange(length, dtype=np.float64)[:, None]
    columns = np.arange(length, dtype=np.float64)[None, :]
    matrix = np.cos(np.pi * (columns + 0.5) * rows / length) * np.sqrt(2.0 / length)
    matrix[0] *= np.sqrt(0.5)
    return matrix


def spread_table(levels, tracers, groups, padded):
    own = levels // groups
    table = cosine_table(levels).reshape(levels, groups, own)
    wide = np.zeros((tracers, levels, groups, padded))
    for t in range(tracers):
        wide[t, :, :, t * own : (t + 1) * own] = table
    wide = wide.reshape(levels * tracers, groups * padded).astype(np.float32)
    high = wide.astype(ml_dtypes.bfloat16)
    low = (wide - high.astype(np.float32)).astype(ml_dtypes.bfloat16)
    return high, low


def halves(x):
    high = x.astype(jnp.bfloat16)
    low = (x - high.astype(jnp.float32)).astype(jnp.bfloat16)
    return high, low


def build(links, weights, merged, w_high, w_low, first, count, blocks, base=0, shift=0):
    slots = links.shape[0]
    groups = -(-blocks // SUB)

    def column(tile, _):
        cols = pl.ds(pl.multiple_of(first + tile * LANES, LANES), LANES)
        into = pl.ds(pl.multiple_of(first + shift + tile * LANES, LANES), LANES)
        lane = []
        block = []
        weight = []
        for k in range(slots):
            link = jnp.broadcast_to(links[k : k + 1, cols], (SUB, LANES))
            lane.append(link & (LANES - 1))
            block.append((link >> 7) - base)
            weight.append(jnp.broadcast_to(weights[k : k + 1, cols], (SUB, LANES)))
        which = lax.broadcasted_iota(jnp.int32, (SUB, LANES), 0)
        for g in range(groups):
            placed = []
            for k in range(slots):
                mine = jnp.where(block[k] == which + g * SUB, weight[k], 0.0)
                total = mine
                for j in range(k):
                    total = total + jnp.where(lane[j] == lane[k], placed[j], 0.0)
                placed.append(mine)
                merged[k, g * SUB : (g + 1) * SUB, :] = total
        lane2 = [jnp.concatenate([v, v], axis=0) for v in lane]

        def strip(s, _):
            rows16 = lax.broadcasted_iota(jnp.int32, (2 * SUB, LANES), 0) + s * (2 * SUB)
            masks = [lane2[k] == rows16 for k in range(slots)]
            for b in range(blocks):
                total = jnp.zeros((2 * SUB, LANES), jnp.float32)
                for k in range(slots):
                    row = jnp.broadcast_to(merged[k, b : b + 1, :], (2 * SUB, LANES))
                    total = jnp.where(masks[k], row, total)
                high, low = halves(total)
                place = pl.ds(pl.multiple_of(b * LANES + s * (2 * SUB), 2 * SUB), 2 * SUB)
                w_high[place, into] = high
                w_low[place, into] = low
            return 0

        lax.fori_loop(0, LANES // (2 * SUB), strip, 0)
        return 0

    lax.fori_loop(0, count // LANES, column, 0)


def picked(source, start, blocks, index, out):
    lane = jnp.broadcast_to(index & (LANES - 1), (SUB, LANES))
    block = jnp.broadcast_to(index >> 7, (SUB, LANES))
    for r in range(source.shape[0] // SUB):
        rows = slice(r * SUB, (r + 1) * SUB)
        got = None
        for b in range(blocks):
            cols = slice(start + b * LANES, start + (b + 1) * LANES)
            t = jnp.take_along_axis(source[rows, cols], lane, axis=1)
            got = t if got is None else jnp.where(block == b, t, got)
        out[rows, :] = got


def put(ext, padded, at, value):
    high, low = halves(value)
    width = value.shape[1]
    ext[0:padded, at : at + width] = high
    ext[padded : 2 * padded, at : at + width] = low


def product(ext, padded, span, w_high, w_low, cols):
    k = slice(*span)
    both = jnp.dot(ext[:, k], w_high[k, cols], preferred_element_type=jnp.float32)
    rest = jnp.dot(ext[0:padded, k], w_low[k, cols], preferred_element_type=jnp.float32)
    return both[0:padded] + both[padded : 2 * padded] + rest


def small(value, m_high, m_low):
    padded = value.shape[0]
    high, low = halves(value)
    both = jnp.concatenate([high, low], axis=0)
    both = jnp.dot(both, m_high, preferred_element_type=jnp.float32)
    rest = jnp.dot(high, m_low, preferred_element_type=jnp.float32)
    return both[0:padded] + both[padded : 2 * padded] + rest


def body(
    n_patch, n_lev, levels,
    field, sc1, sd1, sc2, sd2, pl1, pw1, ul1, uw1, pl2, pw2, ul2, uw2,
    gathered,
    xs, ext, merged, p1h, p1l, u1h, u1l, p2h, p2l, u2h, u2l,
    det1, sm1, det2, sm2, hsend, hrecv,
    ext2, glink, gweight, rlink, rweight, mh, ml, part, full1, full2, done,
    ms_sem, mr_sem,
    hs_sem, hr_sem, as_sem, ar_sem,
):
    tracers, own, cells = field.shape
    rows = own * tracers
    padded = xs.shape[0]
    n1 = cells // 2
    n2 = cells // 4
    halo1 = sc1.shape[2]
    halo2 = sc2.shape[2]
    chunk = cells // n_lev
    me = lax.axis_index("lev")
    patch = lax.axis_index("patch")
    left = lax.rem(patch + n_patch - 1, n_patch)
    right = lax.rem(patch + 1, n_patch)

    barrier = pltpu.get_barrier_semaphore()
    for neighbour in (left, right):
        pl.semaphore_signal(barrier, inc=1, device_id={"patch": neighbour}, device_id_type=MESH)
    for d in range(1, n_lev):
        pl.semaphore_signal(
            barrier, inc=1, device_id={"lev": lax.rem(me + d, n_lev)}, device_id_type=MESH
        )

    if padded > rows:
        edge = rows // SUB * SUB
        xs[edge:padded, :] = jnp.zeros((padded - edge, cells), jnp.float32)
    for t in range(tracers):
        xs[t * own : (t + 1) * own, :] = field[t]

    def copy_to(phase, side):
        return pltpu.make_async_remote_copy(
            src_ref=hsend.at[phase, side],
            dst_ref=hrecv.at[phase, side],
            send_sem=hs_sem.at[phase, side],
            recv_sem=hr_sem.at[phase, side],
            device_id={"patch": left if side else right},
            device_id_type=MESH,
        )

    def meta_to(side):
        return [
            pltpu.make_async_remote_copy(
                src_ref=mine.at[side],
                dst_ref=theirs.at[side],
                send_sem=ms_sem.at[which, side],
                recv_sem=mr_sem.at[which, side],
                device_id={"patch": left if side else right},
                device_id_type=MESH,
            )
            for which, (mine, theirs) in enumerate(((glink, rlink), (gweight, rweight)))
        ]

    def both_sides(step):
        @pl.when(patch == 0)
        def _():
            step(1)
            step(0)

        @pl.when(patch != 0)
        def _():
            step(0)
            step(1)

    outgoing = []

    def scatter(source, base):
        for piece in range(source.shape[1] // chunk):
            d = base // chunk + piece
            part = source.at[:, piece * chunk : (piece + 1) * chunk]
            copy = pltpu.make_async_remote_copy(
                src_ref=part,
                dst_ref=gathered.at[me],
                send_sem=as_sem.at[d],
                recv_sem=ar_sem.at[me],
                device_id={"lev": d},
                device_id_type=MESH,
            )
            outgoing.append((d, copy))

            @pl.when(me != d)
            def _():
                copy.start()

            @pl.when(me == d)
            def _():
                gathered[d] = part[...]

    b1 = n1 // LANES
    b2 = n2 // LANES
    e1 = n1 + 2 * halo1
    e2 = n2 + 2 * halo2
    wide = 256

    def predict(into, start, values, depth, w_high, w_low, n, add):
        for c in range(0, n, wide):
            cols = slice(start + c, start + c + wide)
            source = ext if n1 <= w_high.shape[1] else ext2
            got = product(source, padded, depth, w_high, w_low, cols)
            old = values(cols)
            into[:, cols] = old + got if add else old - got

    def fine1(cols):
        return xs[:, cols]

    def coarse1(cols):
        return xs[:, n1 + cols.start : n1 + cols.stop]

    def fine2(cols):
        return sm1[:, cols]

    def coarse2(cols):
        return sm1[:, n2 + cols.start : n2 + cols.stop]

    def held(ref):
        return lambda cols: ref[:, cols]

    h1 = 2 * halo1 // LANES
    h2 = 2 * halo2 // LANES
    lower = lax.broadcasted_iota(jnp.int32, (padded, LANES), 1) < halo2

    def tail(phase, side):
        if phase == 2:
            return slice(0, LANES)
        return slice(side * LANES, (side + 1) * LANES)

    def sided(phase, side, value):
        if phase != 2:
            return value
        return jnp.where(lower, value, 0.0) if side == 0 else jnp.where(lower, 0.0, value)

    def halo_part(phase, side, column, value):
        cols = slice(column * LANES, (column + 1) * LANES)
        k = tail(phase, side)
        return small(sided(phase, side, value), mh[phase, k, cols], ml[phase, k, cols])

    def two(send):
        return jnp.concatenate([send[0, 1:2, :], send[0, 0:1, :]], axis=1)

    def share(phase, links, weights, start, blocks, indices):
        for side, index in enumerate(indices):
            picked(links, start, blocks, index, glink.at[side, phase])
            picked(weights, start, blocks, index, gweight.at[side, phase])

    picked(xs, n1, b1, sc1[0, 1:2, :], hsend.at[0, 0])
    picked(xs, n1, b1, sc1[0, 0:1, :], hsend.at[0, 1])
    share(0, pl1, pw1, 0, b1, (sd1[0, 1:2, :], sd1[0, 0:1, :]))
    share(1, ul1, uw1, n2, b2, (two(sc2), two(sc2)))
    share(2, pl2, pw2, 0, b2, (two(sd2), two(sd2)))
    put(ext, padded, 0, xs[:, n1:cells])
    build(pl1, pw1, merged, p1h, p1l, 0, n1, e1 // LANES)
    predict(det1, 0, fine1, (0, n1), p1h, p1l, n1, False)
    picked(det1, 0, b1, sd1[0, 1:2, :], part.at[0])
    picked(det1, 0, b1, sd1[0, 0:1, :], part.at[1])

    def spread(links, weights, phase, column, blocks, base):
        build(
            links, weights, merged, mh.at[phase], ml.at[phase], 0, LANES, blocks, base,
            column * LANES,
        )

    for side in range(2):
        spread(glink.at[side, 0], gweight.at[side, 0], 0, side, h1, b1)
    build(ul1, uw1, merged, u1h, u1l, n2, n2, e1 // LANES)
    pl.semaphore_wait(barrier, 2 + n_lev - 1)
    for side in range(2):
        copy_to(0, side).start()
    for side in range(2):
        for c in meta_to(side):
            c.start()
    spread(glink.at[0, 1], gweight.at[0, 1], 1, 0, h1, b1)
    spread(glink.at[0, 2], gweight.at[0, 2], 2, 0, h2, b2)
    build(pl2, pw2, merged, p2h, p2l, 0, n2, e2 // LANES)

    def step0(side):
        copy_to(0, side).wait_recv()
        hsend[1, side] = part[side] - halo_part(0, side, side, hrecv[0, side])
        copy_to(1, side).start()

    both_sides(step0)
    put(ext, padded, n1, hrecv[0, 0])
    put(ext, padded, n1 + halo1, hrecv[0, 1])
    predict(det1, 0, held(det1), (n1, e1), p1h, p1l, n1, False)
    scatter(det1, 0)

    put(ext, padded, 0, det1[...])
    predict(sm1, n2, coarse1, (0, n1), u1h, u1l, n2, True)
    picked(sm1, n2, b2, two(sc2), part.at[0])
    picked(det1, 0, b1, sd1[0, 1:2, :], full1.at[0])
    picked(det1, 0, b1, sd1[0, 0:1, :], full1.at[1])
    for side in range(2):
        for c in meta_to(side):
            c.wait_recv()
    for side in range(2):
        spread(rlink.at[side, 0], rweight.at[side, 0], 0, 2 + side, h1, b1)

    def step1(side):
        copy_to(1, side).wait_recv()
        value = hrecv[1, side] - halo_part(0, 1 - side, 2 + side, hsend[0, 1 - side])
        done[side] = value
        hsend[2, side] = part[0] + halo_part(1, side, 0, value)
        copy_to(2, side).start()

    both_sides(step1)
    put(ext, padded, n1, done[0])
    put(ext, padded, n1 + halo1, done[1])
    predict(sm1, n2, held(sm1), (n1, e1), u1h, u1l, n2, True)

    build(ul1, uw1, merged, u1h, u1l, 0, n2, e1 // LANES)
    predict(sm1, 0, coarse1, (0, e1), u1h, u1l, n2, True)
    put(ext2, padded, 0, sm1[:, n2:n1])
    picked(sm1, n2, b2, two(sc2), full2)
    predict(det2, 0, fine2, (0, n2), p2h, p2l, n2, False)
    picked(det2, 0, b2, two(sd2), part.at[1])
    for side in range(2):
        spread(rlink.at[side, 1], rweight.at[side, 1], 1, 2 + side, h1, b1)

    def step2(side):
        copy_to(2, side).wait_recv()
        value = hrecv[2, side] + halo_part(1, 1 - side, 2 + side, full1[1 - side])
        done[side] = value
        hsend[3, side] = part[1] - halo_part(2, side, 0, value)
        copy_to(3, side).start()

    both_sides(step2)
    put(ext2, padded, n2, jnp.where(lower, done[0], done[1]))
    predict(det2, 0, held(det2), (n2, e2), p2h, p2l, n2, False)
    scatter(det2, n1)

    put(ext2, padded, 0, det2[...])
    for side in range(2):
        spread(rlink.at[side, 2], rweight.at[side, 2], 2, 2 + side, h2, b2)
    build(ul2, uw2, merged, u2h, u2l, 0, n2, e2 // LANES)
    predict(sm2, 0, coarse2, (0, n2), u2h, u2l, n2, True)

    def step3(side):
        copy_to(3, side).wait_recv()
        done[side] = hrecv[3, side] - halo_part(2, 1 - side, 2 + side, full2[...])

    both_sides(step3)
    put(ext2, padded, n2, jnp.where(lower, done[0], done[1]))
    predict(sm2, 0, held(sm2), (n2, e2), u2h, u2l, n2, True)
    scatter(sm2, n1 + n2)

    for s in range(n_lev):

        @pl.when(me != s)
        def _():
            pltpu.make_async_remote_copy(
                src_ref=gathered.at[s],
                dst_ref=gathered.at[s],
                send_sem=as_sem.at[s],
                recv_sem=ar_sem.at[s],
                device_id={"lev": s},
                device_id_type=MESH,
            ).wait_recv()

    for side in range(2):
        for phase in range(4):
            copy_to(phase, side).wait_send()
        for c in meta_to(side):
            c.wait_send()
    for d, copy in outgoing:

        @pl.when(me != d)
        def _():
            copy.wait_send()


def transform(gathered, t_high, t_low, out):
    groups, padded, chunk = gathered.shape
    tracers, levels, _ = out.shape
    high, low = halves(gathered[...].reshape(groups * padded, chunk))
    for t in range(tracers):
        rows = slice(t * levels, (t + 1) * levels)
        out[t] = (
            jnp.dot(t_high[rows, :], high, preferred_element_type=jnp.float32)
            + jnp.dot(t_high[rows, :], low, preferred_element_type=jnp.float32)
            + jnp.dot(t_low[rows, :], high, preferred_element_type=jnp.float32)
        )


def on_device(n_patch, n_lev, *args):
    field, sc1 = args[0], args[1]
    own, tracers, cells = field.shape
    levels = own * n_lev
    rows = own * tracers
    padded = -(-rows // (2 * SUB)) * (2 * SUB)
    n1, n2 = cells // 2, cells // 4
    e1 = n1 + 2 * sc1.shape[2]
    e2 = n2 + 2 * args[3].shape[2]
    chunk = cells // n_lev
    slots = args[5].shape[0]
    t_high, t_low = spread_table(levels, tracers, n_lev, padded)
    f32, bf16 = jnp.float32, jnp.bfloat16
    gathered = pl.pallas_call(
        functools.partial(body, n_patch, n_lev, levels),
        out_shape=jax.ShapeDtypeStruct((n_lev, padded, chunk), f32),
        in_specs=[pl.BlockSpec(memory_space=pltpu.VMEM)] * 13,
        out_specs=pl.BlockSpec(memory_space=pltpu.VMEM),
        scratch_shapes=[
            pltpu.VMEM((padded, cells), f32),
            pltpu.VMEM((2 * padded, e1), bf16),
            pltpu.VMEM((slots, -(-(e1 // LANES) // SUB) * SUB, LANES), f32),
            pltpu.VMEM((e1, n1), bf16),
            pltpu.VMEM((e1, n1), bf16),
            pltpu.VMEM((e1, n1), bf16),
            pltpu.VMEM((e1, n1), bf16),
            pltpu.VMEM((e2, n2), bf16),
            pltpu.VMEM((e2, n2), bf16),
            pltpu.VMEM((e2, n2), bf16),
            pltpu.VMEM((e2, n2), bf16),
            pltpu.VMEM((padded, n1), f32),
            pltpu.VMEM((padded, n1), f32),
            pltpu.VMEM((padded, n2), f32),
            pltpu.VMEM((padded, n2), f32),
            pltpu.VMEM((4, 2, padded, LANES), f32),
            pltpu.VMEM((4, 2, padded, LANES), f32),
            pltpu.VMEM((2 * padded, e2), bf16),
            pltpu.VMEM((2, 3, slots, LANES), jnp.int32),
            pltpu.VMEM((2, 3, slots, LANES), f32),
            pltpu.VMEM((2, 3, slots, LANES), jnp.int32),
            pltpu.VMEM((2, 3, slots, LANES), f32),
            pltpu.VMEM((3, 2 * LANES, 4 * LANES), bf16),
            pltpu.VMEM((3, 2 * LANES, 4 * LANES), bf16),
            pltpu.VMEM((2, padded, LANES), f32),
            pltpu.VMEM((2, padded, LANES), f32),
            pltpu.VMEM((padded, LANES), f32),
            pltpu.VMEM((2, padded, LANES), f32),
            pltpu.SemaphoreType.DMA((2, 2)),
            pltpu.SemaphoreType.DMA((2, 2)),
            pltpu.SemaphoreType.DMA((4, 2)),
            pltpu.SemaphoreType.DMA((4, 2)),
            pltpu.SemaphoreType.DMA((n_lev,)),
            pltpu.SemaphoreType.DMA((n_lev,)),
        ],
        compiler_params=pltpu.CompilerParams(collective_id=0, has_side_effects=True),
    )(jnp.transpose(field, (1, 0, 2)), *args[1:])
    result = pl.pallas_call(
        transform,
        out_shape=jax.ShapeDtypeStruct((tracers, levels, chunk), f32),
        in_specs=[pl.BlockSpec(memory_space=pltpu.VMEM)] * 3,
        out_specs=pl.BlockSpec(memory_space=pltpu.VMEM),
    )(gathered, jnp.asarray(t_high), jnp.asarray(t_low))
    return jnp.transpose(result, (1, 0, 2))


def solution(mesh):
    in_specs = (P("lev", None, "patch"),)
    in_specs += (P("patch", None, None),) * 4
    in_specs += (P(None, "patch"),) * 8
    out_specs = P(None, None, ("patch", "lev"))
    fn = functools.partial(on_device, mesh.shape["patch"], mesh.shape["lev"])
    return jax.shard_map(
        fn, mesh=mesh, in_specs=in_specs, out_specs=out_specs, check_vma=False
    )
```

```python
import functools

import jax
import jax.numpy as jnp
import ml_dtypes
import numpy as np
from jax import lax
from jax.experimental import pallas as pl
from jax.experimental.pallas import tpu as pltpu
from jax.sharding import PartitionSpec as P

LANES = 128
SUB = 8
MESH = pl.DeviceIdType.MESH


def cosine_table(length):
    rows = np.arange(length, dtype=np.float64)[:, None]
    columns = np.arange(length, dtype=np.float64)[None, :]
    matrix = np.cos(np.pi * (columns + 0.5) * rows / length) * np.sqrt(2.0 / length)
    matrix[0] *= np.sqrt(0.5)
    return matrix


def spread_table(levels, tracers, groups, padded):
    own = levels // groups
    table = cosine_table(levels).reshape(levels, groups, own)
    wide = np.zeros((tracers, levels, groups, padded))
    for t in range(tracers):
        wide[t, :, :, t * own : (t + 1) * own] = table
    wide = wide.reshape(levels * tracers, groups * padded).astype(np.float32)
    high = wide.astype(ml_dtypes.bfloat16)
    low = (wide - high.astype(np.float32)).astype(ml_dtypes.bfloat16)
    return high, low


def halves(x):
    high = x.astype(jnp.bfloat16)
    low = (x - high.astype(jnp.float32)).astype(jnp.bfloat16)
    return high, low


def build(links, weights, merged, w_high, w_low, first, count, blocks, base=0, shift=0):
    slots = links.shape[0]
    groups = -(-blocks // SUB)

    def column(tile, _):
        cols = pl.ds(pl.multiple_of(first + tile * LANES, LANES), LANES)
        into = pl.ds(pl.multiple_of(first + shift + tile * LANES, LANES), LANES)
        lane = []
        block = []
        weight = []
        for k in range(slots):
            link = jnp.broadcast_to(links[k : k + 1, cols], (SUB, LANES))
            lane.append(link & (LANES - 1))
            block.append((link >> 7) - base)
            weight.append(jnp.broadcast_to(weights[k : k + 1, cols], (SUB, LANES)))
        which = lax.broadcasted_iota(jnp.int32, (SUB, LANES), 0)
        for g in range(groups):
            placed = []
            for k in range(slots):
                mine = jnp.where(block[k] == which + g * SUB, weight[k], 0.0)
                total = mine
                for j in range(k):
                    total = total + jnp.where(lane[j] == lane[k], placed[j], 0.0)
                placed.append(mine)
                merged[k, g * SUB : (g + 1) * SUB, :] = total
        lane2 = [jnp.concatenate([v, v], axis=0) for v in lane]

        def strip(s, _):
            rows16 = lax.broadcasted_iota(jnp.int32, (2 * SUB, LANES), 0) + s * (2 * SUB)
            masks = [lane2[k] == rows16 for k in range(slots)]
            for b in range(blocks):
                total = jnp.zeros((2 * SUB, LANES), jnp.float32)
                for k in range(slots):
                    row = jnp.broadcast_to(merged[k, b : b + 1, :], (2 * SUB, LANES))
                    total = jnp.where(masks[k], row, total)
                high, low = halves(total)
                place = pl.ds(pl.multiple_of(b * LANES + s * (2 * SUB), 2 * SUB), 2 * SUB)
                w_high[place, into] = high
                w_low[place, into] = low
            return 0

        lax.fori_loop(0, LANES // (2 * SUB), strip, 0)
        return 0

    lax.fori_loop(0, count // LANES, column, 0)


def picked(source, start, blocks, index, out):
    lane = jnp.broadcast_to(index & (LANES - 1), (SUB, LANES))
    block = jnp.broadcast_to(index >> 7, (SUB, LANES))
    for r in range(source.shape[0] // SUB):
        rows = slice(r * SUB, (r + 1) * SUB)
        got = None
        for b in range(blocks):
            cols = slice(start + b * LANES, start + (b + 1) * LANES)
            t = jnp.take_along_axis(source[rows, cols], lane, axis=1)
            got = t if got is None else jnp.where(block == b, t, got)
        out[rows, :] = got


def put(ext, padded, at, value):
    high, low = halves(value)
    width = value.shape[1]
    ext[0:padded, at : at + width] = high
    ext[padded : 2 * padded, at : at + width] = low


def product(ext, padded, span, w_high, w_low, cols):
    k = slice(*span)
    both = jnp.dot(ext[:, k], w_high[k, cols], preferred_element_type=jnp.float32)
    rest = jnp.dot(ext[0:padded, k], w_low[k, cols], preferred_element_type=jnp.float32)
    return both[0:padded] + both[padded : 2 * padded] + rest


def small(value, m_high, m_low):
    padded = value.shape[0]
    high, low = halves(value)
    both = jnp.concatenate([high, low], axis=0)
    both = jnp.dot(both, m_high, preferred_element_type=jnp.float32)
    rest = jnp.dot(high, m_low, preferred_element_type=jnp.float32)
    return both[0:padded] + both[padded : 2 * padded] + rest


def body(
    n_patch, n_lev, levels,
    field, sc1, sd1, sc2, sd2, pl1, pw1, ul1, uw1, pl2, pw2, ul2, uw2,
    gathered,
    xs, ext, merged, p1h, p1l, u1h, u1l, p2h, p2l, u2h, u2l,
    det1, sm1, det2, sm2, hsend, hrecv,
    ext2, glink, gweight, rlink, rweight, mh, ml, part, full1, full2, done,
    ms_sem, mr_sem,
    hs_sem, hr_sem, as_sem, ar_sem,
):
    tracers, own, cells = field.shape
    rows = own * tracers
    padded = xs.shape[0]
    n1 = cells // 2
    n2 = cells // 4
    halo1 = sc1.shape[2]
    halo2 = sc2.shape[2]
    chunk = cells // n_lev
    me = lax.axis_index("lev")
    patch = lax.axis_index("patch")
    left = lax.rem(patch + n_patch - 1, n_patch)
    right = lax.rem(patch + 1, n_patch)

    barrier = pltpu.get_barrier_semaphore()
    for neighbour in (left, right):
        pl.semaphore_signal(barrier, inc=1, device_id={"patch": neighbour}, device_id_type=MESH)
    for d in range(1, n_lev):
        pl.semaphore_signal(
            barrier, inc=1, device_id={"lev": lax.rem(me + d, n_lev)}, device_id_type=MESH
        )

    if padded > rows:
        edge = rows // SUB * SUB
        xs[edge:padded, :] = jnp.zeros((padded - edge, cells), jnp.float32)
    for t in range(tracers):
        xs[t * own : (t + 1) * own, :] = field[t]

    def copy_to(phase, side):
        return pltpu.make_async_remote_copy(
            src_ref=hsend.at[phase, side],
            dst_ref=hrecv.at[phase, side],
            send_sem=hs_sem.at[phase, side],
            recv_sem=hr_sem.at[phase, side],
            device_id={"patch": left if side else right},
            device_id_type=MESH,
        )

    def meta_to(side):
        return [
            pltpu.make_async_remote_copy(
                src_ref=mine.at[side],
                dst_ref=theirs.at[side],
                send_sem=ms_sem.at[which, side],
                recv_sem=mr_sem.at[which, side],
                device_id={"patch": left if side else right},
                device_id_type=MESH,
            )
            for which, (mine, theirs) in enumerate(((glink, rlink), (gweight, rweight)))
        ]

    def both_sides(step):
        @pl.when(patch == 0)
        def _():
            step(1)
            step(0)

        @pl.when(patch != 0)
        def _():
            step(0)
            step(1)

    outgoing = []

    def scatter(source, base):
        for piece in range(source.shape[1] // chunk):
            d = base // chunk + piece
            part = source.at[:, piece * chunk : (piece + 1) * chunk]
            copy = pltpu.make_async_remote_copy(
                src_ref=part,
                dst_ref=gathered.at[me],
                send_sem=as_sem.at[d],
                recv_sem=ar_sem.at[me],
                device_id={"lev": d},
                device_id_type=MESH,
            )
            outgoing.append((d, copy))

            @pl.when(me != d)
            def _():
                copy.start()

            @pl.when(me == d)
            def _():
                gathered[d] = part[...]

    b1 = n1 // LANES
    b2 = n2 // LANES
    e1 = n1 + 2 * halo1
    e2 = n2 + 2 * halo2
    wide = 256

    def predict(into, start, values, depth, w_high, w_low, n, add):
        for c in range(0, n, wide):
            cols = slice(start + c, start + c + wide)
            source = ext if n1 <= w_high.shape[1] else ext2
            got = product(source, padded, depth, w_high, w_low, cols)
            old = values(cols)
            into[:, cols] = old + got if add else old - got

    def fine1(cols):
        return xs[:, cols]

    def coarse1(cols):
        return xs[:, n1 + cols.start : n1 + cols.stop]

    def fine2(cols):
        return sm1[:, cols]

    def coarse2(cols):
        return sm1[:, n2 + cols.start : n2 + cols.stop]

    def held(ref):
        return lambda cols: ref[:, cols]

    h1 = 2 * halo1 // LANES
    h2 = 2 * halo2 // LANES
    lower = lax.broadcasted_iota(jnp.int32, (padded, LANES), 1) < halo2

    def tail(phase, side):
        if phase == 2:
            return slice(0, LANES)
        return slice(side * LANES, (side + 1) * LANES)

    def sided(phase, side, value):
        if phase != 2:
            return value
        return jnp.where(lower, value, 0.0) if side == 0 else jnp.where(lower, 0.0, value)

    def halo_part(phase, side, column, value):
        cols = slice(column * LANES, (column + 1) * LANES)
        k = tail(phase, side)
        return small(sided(phase, side, value), mh[phase, k, cols], ml[phase, k, cols])

    def two(send):
        return jnp.concatenate([send[0, 1:2, :], send[0, 0:1, :]], axis=1)

    def share(phase, links, weights, start, blocks, indices):
        for side, index in enumerate(indices):
            picked(links, start, blocks, index, glink.at[side, phase])
            picked(weights, start, blocks, index, gweight.at[side, phase])

    picked(xs, n1, b1, sc1[0, 1:2, :], hsend.at[0, 0])
    picked(xs, n1, b1, sc1[0, 0:1, :], hsend.at[0, 1])
    pl.semaphore_wait(barrier, 2 + n_lev - 1)
    for side in range(2):
        copy_to(0, side).start()
    share(0, pl1, pw1, 0, b1, (sd1[0, 1:2, :], sd1[0, 0:1, :]))
    share(1, ul1, uw1, n2, b2, (two(sc2), two(sc2)))
    share(2, pl2, pw2, 0, b2, (two(sd2), two(sd2)))
    for side in range(2):
        for c in meta_to(side):
            c.start()
    put(ext, padded, 0, xs[:, n1:cells])
    build(pl1, pw1, merged, p1h, p1l, 0, n1, e1 // LANES)
    predict(det1, 0, fine1, (0, n1), p1h, p1l, n1, False)
    picked(det1, 0, b1, sd1[0, 1:2, :], part.at[0])
    picked(det1, 0, b1, sd1[0, 0:1, :], part.at[1])

    def spread(links, weights, phase, column, blocks, base):
        build(
            links, weights, merged, mh.at[phase], ml.at[phase], 0, LANES, blocks, base,
            column * LANES,
        )

    for side in range(2):
        spread(glink.at[side, 0], gweight.at[side, 0], 0, side, h1, b1)

    def step0(side):
        copy_to(0, side).wait_recv()
        hsend[1, side] = part[side] - halo_part(0, side, side, hrecv[0, side])
        copy_to(1, side).start()

    both_sides(step0)
    put(ext, padded, n1, hrecv[0, 0])
    put(ext, padded, n1 + halo1, hrecv[0, 1])
    predict(det1, 0, held(det1), (n1, e1), p1h, p1l, n1, False)
    scatter(det1, 0)

    spread(glink.at[0, 1], gweight.at[0, 1], 1, 0, h1, b1)
    build(ul1, uw1, merged, u1h, u1l, n2, n2, e1 // LANES)
    put(ext, padded, 0, det1[...])
    predict(sm1, n2, coarse1, (0, n1), u1h, u1l, n2, True)
    picked(sm1, n2, b2, two(sc2), part.at[0])
    picked(det1, 0, b1, sd1[0, 1:2, :], full1.at[0])
    picked(det1, 0, b1, sd1[0, 0:1, :], full1.at[1])
    for side in range(2):
        for c in meta_to(side):
            c.wait_recv()
    for side in range(2):
        spread(rlink.at[side, 0], rweight.at[side, 0], 0, 2 + side, h1, b1)

    def step1(side):
        copy_to(1, side).wait_recv()
        value = hrecv[1, side] - halo_part(0, 1 - side, 2 + side, hsend[0, 1 - side])
        done[side] = value
        hsend[2, side] = part[0] + halo_part(1, side, 0, value)
        copy_to(2, side).start()

    both_sides(step1)
    put(ext, padded, n1, done[0])
    put(ext, padded, n1 + halo1, done[1])
    predict(sm1, n2, held(sm1), (n1, e1), u1h, u1l, n2, True)

    spread(glink.at[0, 2], gweight.at[0, 2], 2, 0, h2, b2)
    build(pl2, pw2, merged, p2h, p2l, 0, n2, e2 // LANES)
    build(ul1, uw1, merged, u1h, u1l, 0, n2, e1 // LANES)
    predict(sm1, 0, coarse1, (0, e1), u1h, u1l, n2, True)
    put(ext2, padded, 0, sm1[:, n2:n1])
    picked(sm1, n2, b2, two(sc2), full2)
    predict(det2, 0, fine2, (0, n2), p2h, p2l, n2, False)
    picked(det2, 0, b2, two(sd2), part.at[1])
    for side in range(2):
        spread(rlink.at[side, 1], rweight.at[side, 1], 1, 2 + side, h1, b1)

    def step2(side):
        copy_to(2, side).wait_recv()
        value = hrecv[2, side] + halo_part(1, 1 - side, 2 + side, full1[1 - side])
        done[side] = value
        hsend[3, side] = part[1] - halo_part(2, side, 0, value)
        copy_to(3, side).start()

    both_sides(step2)
    put(ext2, padded, n2, jnp.where(lower, done[0], done[1]))
    predict(det2, 0, held(det2), (n2, e2), p2h, p2l, n2, False)
    scatter(det2, n1)

    put(ext2, padded, 0, det2[...])
    for side in range(2):
        spread(rlink.at[side, 2], rweight.at[side, 2], 2, 2 + side, h2, b2)
    build(ul2, uw2, merged, u2h, u2l, 0, n2, e2 // LANES)
    predict(sm2, 0, coarse2, (0, n2), u2h, u2l, n2, True)

    def step3(side):
        copy_to(3, side).wait_recv()
        done[side] = hrecv[3, side] - halo_part(2, 1 - side, 2 + side, full2[...])

    both_sides(step3)
    put(ext2, padded, n2, jnp.where(lower, done[0], done[1]))
    predict(sm2, 0, held(sm2), (n2, e2), u2h, u2l, n2, True)
    scatter(sm2, n1 + n2)

    for s in range(n_lev):

        @pl.when(me != s)
        def _():
            pltpu.make_async_remote_copy(
                src_ref=gathered.at[s],
                dst_ref=gathered.at[s],
                send_sem=as_sem.at[s],
                recv_sem=ar_sem.at[s],
                device_id={"lev": s},
                device_id_type=MESH,
            ).wait_recv()

    for side in range(2):
        for phase in range(4):
            copy_to(phase, side).wait_send()
        for c in meta_to(side):
            c.wait_send()
    for d, copy in outgoing:

        @pl.when(me != d)
        def _():
            copy.wait_send()


def transform(gathered, t_high, t_low, out):
    groups, padded, chunk = gathered.shape
    tracers, levels, _ = out.shape
    high, low = halves(gathered[...].reshape(groups * padded, chunk))
    for t in range(tracers):
        rows = slice(t * levels, (t + 1) * levels)
        out[t] = (
            jnp.dot(t_high[rows, :], high, preferred_element_type=jnp.float32)
            + jnp.dot(t_high[rows, :], low, preferred_element_type=jnp.float32)
            + jnp.dot(t_low[rows, :], high, preferred_element_type=jnp.float32)
        )


def on_device(n_patch, n_lev, *args):
    field, sc1 = args[0], args[1]
    own, tracers, cells = field.shape
    levels = own * n_lev
    rows = own * tracers
    padded = -(-rows // (2 * SUB)) * (2 * SUB)
    n1, n2 = cells // 2, cells // 4
    e1 = n1 + 2 * sc1.shape[2]
    e2 = n2 + 2 * args[3].shape[2]
    chunk = cells // n_lev
    slots = args[5].shape[0]
    t_high, t_low = spread_table(levels, tracers, n_lev, padded)
    f32, bf16 = jnp.float32, jnp.bfloat16
    gathered = pl.pallas_call(
        functools.partial(body, n_patch, n_lev, levels),
        out_shape=jax.ShapeDtypeStruct((n_lev, padded, chunk), f32),
        in_specs=[pl.BlockSpec(memory_space=pltpu.VMEM)] * 13,
        out_specs=pl.BlockSpec(memory_space=pltpu.VMEM),
        scratch_shapes=[
            pltpu.VMEM((padded, cells), f32),
            pltpu.VMEM((2 * padded, e1), bf16),
            pltpu.VMEM((slots, -(-(e1 // LANES) // SUB) * SUB, LANES), f32),
            pltpu.VMEM((e1, n1), bf16),
            pltpu.VMEM((e1, n1), bf16),
            pltpu.VMEM((e1, n1), bf16),
            pltpu.VMEM((e1, n1), bf16),
            pltpu.VMEM((e2, n2), bf16),
            pltpu.VMEM((e2, n2), bf16),
            pltpu.VMEM((e2, n2), bf16),
            pltpu.VMEM((e2, n2), bf16),
            pltpu.VMEM((padded, n1), f32),
            pltpu.VMEM((padded, n1), f32),
            pltpu.VMEM((padded, n2), f32),
            pltpu.VMEM((padded, n2), f32),
            pltpu.VMEM((4, 2, padded, LANES), f32),
            pltpu.VMEM((4, 2, padded, LANES), f32),
            pltpu.VMEM((2 * padded, e2), bf16),
            pltpu.VMEM((2, 3, slots, LANES), jnp.int32),
            pltpu.VMEM((2, 3, slots, LANES), f32),
            pltpu.VMEM((2, 3, slots, LANES), jnp.int32),
            pltpu.VMEM((2, 3, slots, LANES), f32),
            pltpu.VMEM((3, 2 * LANES, 4 * LANES), bf16),
            pltpu.VMEM((3, 2 * LANES, 4 * LANES), bf16),
            pltpu.VMEM((2, padded, LANES), f32),
            pltpu.VMEM((2, padded, LANES), f32),
            pltpu.VMEM((padded, LANES), f32),
            pltpu.VMEM((2, padded, LANES), f32),
            pltpu.SemaphoreType.DMA((2, 2)),
            pltpu.SemaphoreType.DMA((2, 2)),
            pltpu.SemaphoreType.DMA((4, 2)),
            pltpu.SemaphoreType.DMA((4, 2)),
            pltpu.SemaphoreType.DMA((n_lev,)),
            pltpu.SemaphoreType.DMA((n_lev,)),
        ],
        compiler_params=pltpu.CompilerParams(collective_id=0, has_side_effects=True),
    )(jnp.transpose(field, (1, 0, 2)), *args[1:])
    result = pl.pallas_call(
        transform,
        out_shape=jax.ShapeDtypeStruct((tracers, levels, chunk), f32),
        in_specs=[pl.BlockSpec(memory_space=pltpu.VMEM)] * 3,
        out_specs=pl.BlockSpec(memory_space=pltpu.VMEM),
    )(gathered, jnp.asarray(t_high), jnp.asarray(t_low))
    return jnp.transpose(result, (1, 0, 2))


def solution(mesh):
    in_specs = (P("lev", None, "patch"),)
    in_specs += (P("patch", None, None),) * 4
    in_specs += (P(None, "patch"),) * 8
    out_specs = P(None, None, ("patch", "lev"))
    fn = functools.partial(on_device, mesh.shape["patch"], mesh.shape["lev"])
    return jax.shard_map(
        fn, mesh=mesh, in_specs=in_specs, out_specs=out_specs, check_vma=False
    )
```

```python
import functools

import jax
import jax.numpy as jnp
import ml_dtypes
import numpy as np
from jax import lax
from jax.experimental import pallas as pl
from jax.experimental.pallas import tpu as pltpu
from jax.sharding import PartitionSpec as P

LANES = 128
SUB = 8
MESH = pl.DeviceIdType.MESH


def cosine_table(length):
    rows = np.arange(length, dtype=np.float64)[:, None]
    columns = np.arange(length, dtype=np.float64)[None, :]
    matrix = np.cos(np.pi * (columns + 0.5) * rows / length) * np.sqrt(2.0 / length)
    matrix[0] *= np.sqrt(0.5)
    return matrix


def spread_table(levels, tracers, groups, padded):
    own = levels // groups
    table = cosine_table(levels).reshape(levels, groups, own)
    wide = np.zeros((tracers, levels, groups, padded))
    for t in range(tracers):
        wide[t, :, :, t * own : (t + 1) * own] = table
    wide = wide.reshape(levels * tracers, groups * padded).astype(np.float32)
    high = wide.astype(ml_dtypes.bfloat16)
    low = (wide - high.astype(np.float32)).astype(ml_dtypes.bfloat16)
    return high, low


def halves(x):
    high = x.astype(jnp.bfloat16)
    low = (x - high.astype(jnp.float32)).astype(jnp.bfloat16)
    return high, low


def build(links, weights, merged, w_high, w_low, first, count, blocks, base=0, shift=0):
    slots = links.shape[0]
    groups = -(-blocks // SUB)

    def column(tile, _):
        cols = pl.ds(pl.multiple_of(first + tile * LANES, LANES), LANES)
        into = pl.ds(pl.multiple_of(first + shift + tile * LANES, LANES), LANES)
        lane = []
        block = []
        weight = []
        for k in range(slots):
            link = jnp.broadcast_to(links[k : k + 1, cols], (SUB, LANES))
            lane.append(link & (LANES - 1))
            block.append((link >> 7) - base)
            weight.append(jnp.broadcast_to(weights[k : k + 1, cols], (SUB, LANES)))
        which = lax.broadcasted_iota(jnp.int32, (SUB, LANES), 0)
        for g in range(groups):
            placed = []
            for k in range(slots):
                mine = jnp.where(block[k] == which + g * SUB, weight[k], 0.0)
                total = mine
                for j in range(k):
                    total = total + jnp.where(lane[j] == lane[k], placed[j], 0.0)
                placed.append(mine)
                merged[k, g * SUB : (g + 1) * SUB, :] = total
        lane2 = [jnp.concatenate([v, v], axis=0) for v in lane]

        def strip(s, _):
            rows16 = lax.broadcasted_iota(jnp.int32, (2 * SUB, LANES), 0) + s * (2 * SUB)
            masks = [lane2[k] == rows16 for k in range(slots)]
            for b in range(blocks):
                total = jnp.zeros((2 * SUB, LANES), jnp.float32)
                for k in range(slots):
                    row = jnp.broadcast_to(merged[k, b : b + 1, :], (2 * SUB, LANES))
                    total = jnp.where(masks[k], row, total)
                high, low = halves(total)
                place = pl.ds(pl.multiple_of(b * LANES + s * (2 * SUB), 2 * SUB), 2 * SUB)
                w_high[place, into] = high
                w_low[place, into] = low
            return 0

        lax.fori_loop(0, LANES // (2 * SUB), strip, 0)
        return 0

    lax.fori_loop(0, count // LANES, column, 0)


def picked(source, start, blocks, index, out):
    lane = jnp.broadcast_to(index & (LANES - 1), (SUB, LANES))
    block = jnp.broadcast_to(index >> 7, (SUB, LANES))
    for r in range(source.shape[0] // SUB):
        rows = slice(r * SUB, (r + 1) * SUB)
        got = None
        for b in range(blocks):
            cols = slice(start + b * LANES, start + (b + 1) * LANES)
            t = jnp.take_along_axis(source[rows, cols], lane, axis=1)
            got = t if got is None else jnp.where(block == b, t, got)
        out[rows, :] = got


def put(ext, padded, at, value):
    high, low = halves(value)
    width = value.shape[1]
    ext[0:padded, at : at + width] = high
    ext[padded : 2 * padded, at : at + width] = low


def product(ext, padded, span, w_high, w_low, cols):
    k = slice(*span)
    both = jnp.dot(ext[:, k], w_high[k, cols], preferred_element_type=jnp.float32)
    rest = jnp.dot(ext[0:padded, k], w_low[k, cols], preferred_element_type=jnp.float32)
    return both[0:padded] + both[padded : 2 * padded] + rest


def small(value, m_high, m_low):
    padded = value.shape[0]
    high, low = halves(value)
    both = jnp.concatenate([high, low], axis=0)
    both = jnp.dot(both, m_high, preferred_element_type=jnp.float32)
    rest = jnp.dot(high, m_low, preferred_element_type=jnp.float32)
    return both[0:padded] + both[padded : 2 * padded] + rest


def body(
    n_patch, n_lev, levels,
    field, sc1, sd1, sc2, sd2, pl1, pw1, ul1, uw1, pl2, pw2, ul2, uw2,
    gathered,
    xs, ext, merged, p1h, p1l, u1h, u1l, p2h, p2l, u2h, u2l,
    det1, sm1, det2, sm2, hsend, hrecv,
    ext2, glink, gweight, rlink, rweight, mh, ml, part, full1, full2, done,
    ms_sem, mr_sem,
    hs_sem, hr_sem, as_sem, ar_sem,
):
    tracers, own, cells = field.shape
    rows = own * tracers
    padded = xs.shape[0]
    n1 = cells // 2
    n2 = cells // 4
    halo1 = sc1.shape[2]
    halo2 = sc2.shape[2]
    chunk = cells // n_lev
    me = lax.axis_index("lev")
    patch = lax.axis_index("patch")
    left = lax.rem(patch + n_patch - 1, n_patch)
    right = lax.rem(patch + 1, n_patch)

    barrier = pltpu.get_barrier_semaphore()
    for neighbour in (left, right):
        pl.semaphore_signal(barrier, inc=1, device_id={"patch": neighbour}, device_id_type=MESH)
    for d in range(1, n_lev):
        pl.semaphore_signal(
            barrier, inc=1, device_id={"lev": lax.rem(me + d, n_lev)}, device_id_type=MESH
        )

    if padded > rows:
        edge = rows // SUB * SUB
        xs[edge:padded, :] = jnp.zeros((padded - edge, cells), jnp.float32)
    for t in range(tracers):
        xs[t * own : (t + 1) * own, :] = field[t]

    def copy_to(phase, side):
        return pltpu.make_async_remote_copy(
            src_ref=hsend.at[phase, side],
            dst_ref=hrecv.at[phase, side],
            send_sem=hs_sem.at[phase, side],
            recv_sem=hr_sem.at[phase, side],
            device_id={"patch": left if side else right},
            device_id_type=MESH,
        )

    def meta_to(side):
        return [
            pltpu.make_async_remote_copy(
                src_ref=mine.at[side],
                dst_ref=theirs.at[side],
                send_sem=ms_sem.at[which, side],
                recv_sem=mr_sem.at[which, side],
                device_id={"patch": left if side else right},
                device_id_type=MESH,
            )
            for which, (mine, theirs) in enumerate(((glink, rlink), (gweight, rweight)))
        ]

    def both_sides(step):
        @pl.when(patch == 0)
        def _():
            step(1)
            step(0)

        @pl.when(patch != 0)
        def _():
            step(0)
            step(1)

    outgoing = []

    def scatter(source, base):
        for piece in range(source.shape[1] // chunk):
            d = base // chunk + piece
            part = source.at[:, piece * chunk : (piece + 1) * chunk]
            copy = pltpu.make_async_remote_copy(
                src_ref=part,
                dst_ref=gathered.at[me],
                send_sem=as_sem.at[d],
                recv_sem=ar_sem.at[me],
                device_id={"lev": d},
                device_id_type=MESH,
            )
            outgoing.append((d, copy))

            @pl.when(me != d)
            def _():
                copy.start()

            @pl.when(me == d)
            def _():
                gathered[d] = part[...]

    b1 = n1 // LANES
    b2 = n2 // LANES
    e1 = n1 + 2 * halo1
    e2 = n2 + 2 * halo2
    wide = 256

    def predict(into, start, values, depth, w_high, w_low, n, add):
        for c in range(0, n, wide):
            cols = slice(start + c, start + c + wide)
            source = ext if n1 <= w_high.shape[1] else ext2
            got = product(source, padded, depth, w_high, w_low, cols)
            old = values(cols)
            into[:, cols] = old + got if add else old - got

    def fine1(cols):
        return xs[:, cols]

    def coarse1(cols):
        return xs[:, n1 + cols.start : n1 + cols.stop]

    def fine2(cols):
        return sm1[:, cols]

    def coarse2(cols):
        return sm1[:, n2 + cols.start : n2 + cols.stop]

    def held(ref):
        return lambda cols: ref[:, cols]

    h1 = 2 * halo1 // LANES
    h2 = 2 * halo2 // LANES
    lower = lax.broadcasted_iota(jnp.int32, (padded, LANES), 1) < halo2

    def tail(phase, side):
        if phase == 2:
            return slice(0, LANES)
        return slice(side * LANES, (side + 1) * LANES)

    def sided(phase, side, value):
        if phase != 2:
            return value
        return jnp.where(lower, value, 0.0) if side == 0 else jnp.where(lower, 0.0, value)

    def halo_part(phase, side, column, value):
        cols = slice(column * LANES, (column + 1) * LANES)
        k = tail(phase, side)
        return small(sided(phase, side, value), mh[phase, k, cols], ml[phase, k, cols])

    def two(send):
        return jnp.concatenate([send[0, 1:2, :], send[0, 0:1, :]], axis=1)

    def share(phase, links, weights, start, blocks, indices):
        for side, index in enumerate(indices):
            picked(links, start, blocks, index, glink.at[side, phase])
            picked(weights, start, blocks, index, gweight.at[side, phase])

    picked(xs, n1, b1, sc1[0, 1:2, :], hsend.at[0, 0])
    picked(xs, n1, b1, sc1[0, 0:1, :], hsend.at[0, 1])
    pl.semaphore_wait(barrier, 2 + n_lev - 1)
    for side in range(2):
        copy_to(0, side).start()
    share(0, pl1, pw1, 0, b1, (sd1[0, 1:2, :], sd1[0, 0:1, :]))
    share(1, ul1, uw1, n2, b2, (two(sc2), two(sc2)))
    share(2, pl2, pw2, 0, b2, (two(sd2), two(sd2)))
    for side in range(2):
        for c in meta_to(side):
            c.start()
    put(ext, padded, 0, xs[:, n1:cells])
    build(pl1, pw1, merged, p1h, p1l, 0, n1, e1 // LANES)
    predict(det1, 0, fine1, (0, n1), p1h, p1l, n1, False)
    picked(det1, 0, b1, sd1[0, 1:2, :], part.at[0])
    picked(det1, 0, b1, sd1[0, 0:1, :], part.at[1])

    def spread(links, weights, phase, column, blocks, base):
        build(
            links, weights, merged, mh.at[phase], ml.at[phase], 0, LANES, blocks, base,
            column * LANES,
        )

    for side in range(2):
        spread(glink.at[side, 0], gweight.at[side, 0], 0, side, h1, b1)

    def step0(side):
        copy_to(0, side).wait_recv()
        hsend[1, side] = part[side] - halo_part(0, side, side, hrecv[0, side])
        copy_to(1, side).start()

    both_sides(step0)
    put(ext, padded, n1, hrecv[0, 0])
    put(ext, padded, n1 + halo1, hrecv[0, 1])
    predict(det1, 0, held(det1), (n1, e1), p1h, p1l, n1, False)
    scatter(det1, 0)

    spread(glink.at[0, 1], gweight.at[0, 1], 1, 0, h1, b1)
    build(ul1, uw1, merged, u1h, u1l, n2, n2, e1 // LANES)
    put(ext, padded, 0, det1[...])
    predict(sm1, n2, coarse1, (0, n1), u1h, u1l, n2, True)
    picked(sm1, n2, b2, two(sc2), part.at[0])
    picked(det1, 0, b1, sd1[0, 1:2, :], full1.at[0])
    picked(det1, 0, b1, sd1[0, 0:1, :], full1.at[1])
    for side in range(2):
        for c in meta_to(side):
            c.wait_recv()
    for side in range(2):
        spread(rlink.at[side, 0], rweight.at[side, 0], 0, 2 + side, h1, b1)
    spread(glink.at[0, 2], gweight.at[0, 2], 2, 0, h2, b2)
    build(pl2, pw2, merged, p2h, p2l, 0, n2, e2 // LANES)
    for side in range(2):
        spread(rlink.at[side, 1], rweight.at[side, 1], 1, 2 + side, h1, b1)

    def step1(side):
        copy_to(1, side).wait_recv()
        value = hrecv[1, side] - halo_part(0, 1 - side, 2 + side, hsend[0, 1 - side])
        done[side] = value
        hsend[2, side] = part[0] + halo_part(1, side, 0, value)
        copy_to(2, side).start()

    both_sides(step1)
    put(ext, padded, n1, done[0])
    put(ext, padded, n1 + halo1, done[1])
    predict(sm1, n2, held(sm1), (n1, e1), u1h, u1l, n2, True)

    build(ul1, uw1, merged, u1h, u1l, 0, n2, e1 // LANES)
    predict(sm1, 0, coarse1, (0, e1), u1h, u1l, n2, True)
    put(ext2, padded, 0, sm1[:, n2:n1])
    picked(sm1, n2, b2, two(sc2), full2)
    predict(det2, 0, fine2, (0, n2), p2h, p2l, n2, False)
    picked(det2, 0, b2, two(sd2), part.at[1])

    def step2(side):
        copy_to(2, side).wait_recv()
        value = hrecv[2, side] + halo_part(1, 1 - side, 2 + side, full1[1 - side])
        done[side] = value
        hsend[3, side] = part[1] - halo_part(2, side, 0, value)
        copy_to(3, side).start()

    both_sides(step2)
    put(ext2, padded, n2, jnp.where(lower, done[0], done[1]))
    predict(det2, 0, held(det2), (n2, e2), p2h, p2l, n2, False)
    scatter(det2, n1)

    put(ext2, padded, 0, det2[...])
    for side in range(2):
        spread(rlink.at[side, 2], rweight.at[side, 2], 2, 2 + side, h2, b2)
    build(ul2, uw2, merged, u2h, u2l, 0, n2, e2 // LANES)
    predict(sm2, 0, coarse2, (0, n2), u2h, u2l, n2, True)

    def step3(side):
        copy_to(3, side).wait_recv()
        done[side] = hrecv[3, side] - halo_part(2, 1 - side, 2 + side, full2[...])

    both_sides(step3)
    put(ext2, padded, n2, jnp.where(lower, done[0], done[1]))
    predict(sm2, 0, held(sm2), (n2, e2), u2h, u2l, n2, True)
    scatter(sm2, n1 + n2)

    for s in range(n_lev):

        @pl.when(me != s)
        def _():
            pltpu.make_async_remote_copy(
                src_ref=gathered.at[s],
                dst_ref=gathered.at[s],
                send_sem=as_sem.at[s],
                recv_sem=ar_sem.at[s],
                device_id={"lev": s},
                device_id_type=MESH,
            ).wait_recv()

    for side in range(2):
        for phase in range(4):
            copy_to(phase, side).wait_send()
        for c in meta_to(side):
            c.wait_send()
    for d, copy in outgoing:

        @pl.when(me != d)
        def _():
            copy.wait_send()


def transform(gathered, t_high, t_low, out):
    groups, padded, chunk = gathered.shape
    tracers, levels, _ = out.shape
    high, low = halves(gathered[...].reshape(groups * padded, chunk))
    for t in range(tracers):
        rows = slice(t * levels, (t + 1) * levels)
        out[t] = (
            jnp.dot(t_high[rows, :], high, preferred_element_type=jnp.float32)
            + jnp.dot(t_high[rows, :], low, preferred_element_type=jnp.float32)
            + jnp.dot(t_low[rows, :], high, preferred_element_type=jnp.float32)
        )


def on_device(n_patch, n_lev, *args):
    field, sc1 = args[0], args[1]
    own, tracers, cells = field.shape
    levels = own * n_lev
    rows = own * tracers
    padded = -(-rows // (2 * SUB)) * (2 * SUB)
    n1, n2 = cells // 2, cells // 4
    e1 = n1 + 2 * sc1.shape[2]
    e2 = n2 + 2 * args[3].shape[2]
    chunk = cells // n_lev
    slots = args[5].shape[0]
    t_high, t_low = spread_table(levels, tracers, n_lev, padded)
    f32, bf16 = jnp.float32, jnp.bfloat16
    gathered = pl.pallas_call(
        functools.partial(body, n_patch, n_lev, levels),
        out_shape=jax.ShapeDtypeStruct((n_lev, padded, chunk), f32),
        in_specs=[pl.BlockSpec(memory_space=pltpu.VMEM)] * 13,
        out_specs=pl.BlockSpec(memory_space=pltpu.VMEM),
        scratch_shapes=[
            pltpu.VMEM((padded, cells), f32),
            pltpu.VMEM((2 * padded, e1), bf16),
            pltpu.VMEM((slots, -(-(e1 // LANES) // SUB) * SUB, LANES), f32),
            pltpu.VMEM((e1, n1), bf16),
            pltpu.VMEM((e1, n1), bf16),
            pltpu.VMEM((e1, n1), bf16),
            pltpu.VMEM((e1, n1), bf16),
            pltpu.VMEM((e2, n2), bf16),
            pltpu.VMEM((e2, n2), bf16),
            pltpu.VMEM((e2, n2), bf16),
            pltpu.VMEM((e2, n2), bf16),
            pltpu.VMEM((padded, n1), f32),
            pltpu.VMEM((padded, n1), f32),
            pltpu.VMEM((padded, n2), f32),
            pltpu.VMEM((padded, n2), f32),
            pltpu.VMEM((4, 2, padded, LANES), f32),
            pltpu.VMEM((4, 2, padded, LANES), f32),
            pltpu.VMEM((2 * padded, e2), bf16),
            pltpu.VMEM((2, 3, slots, LANES), jnp.int32),
            pltpu.VMEM((2, 3, slots, LANES), f32),
            pltpu.VMEM((2, 3, slots, LANES), jnp.int32),
            pltpu.VMEM((2, 3, slots, LANES), f32),
            pltpu.VMEM((3, 2 * LANES, 4 * LANES), bf16),
            pltpu.VMEM((3, 2 * LANES, 4 * LANES), bf16),
            pltpu.VMEM((2, padded, LANES), f32),
            pltpu.VMEM((2, padded, LANES), f32),
            pltpu.VMEM((padded, LANES), f32),
            pltpu.VMEM((2, padded, LANES), f32),
            pltpu.SemaphoreType.DMA((2, 2)),
            pltpu.SemaphoreType.DMA((2, 2)),
            pltpu.SemaphoreType.DMA((4, 2)),
            pltpu.SemaphoreType.DMA((4, 2)),
            pltpu.SemaphoreType.DMA((n_lev,)),
            pltpu.SemaphoreType.DMA((n_lev,)),
        ],
        compiler_params=pltpu.CompilerParams(collective_id=0, has_side_effects=True),
    )(jnp.transpose(field, (1, 0, 2)), *args[1:])
    result = pl.pallas_call(
        transform,
        out_shape=jax.ShapeDtypeStruct((tracers, levels, chunk), f32),
        in_specs=[pl.BlockSpec(memory_space=pltpu.VMEM)] * 3,
        out_specs=pl.BlockSpec(memory_space=pltpu.VMEM),
    )(gathered, jnp.asarray(t_high), jnp.asarray(t_low))
    return jnp.transpose(result, (1, 0, 2))


def solution(mesh):
    in_specs = (P("lev", None, "patch"),)
    in_specs += (P("patch", None, None),) * 4
    in_specs += (P(None, "patch"),) * 8
    out_specs = P(None, None, ("patch", "lev"))
    fn = functools.partial(on_device, mesh.shape["patch"], mesh.shape["lev"])
    return jax.shard_map(
        fn, mesh=mesh, in_specs=in_specs, out_specs=out_specs, check_vma=False
    )
```
